32 devices in a mesh: tm: 2 (over x), space: 16 (over z, y, core).
Axes of the slice: x: 2, y: 2, z: 4, core: 2. Of those that a mesh axis runs over, the one named last changes fastest.
Arguments:
- queries: bfloat16 [12288, 2240], P(('tm', 'space')), may hold values from -6 to 6
- keys: bfloat16 [12288, 2240], P(('tm', 'space')), may hold values from -6 to 6
- values: bfloat16 [12288, 2240], P(('tm', 'space')), may hold values from -6 to 6
- out_grad: bfloat16 [12288, 2240], P(('tm', 'space')), may hold values from -2560 to 2560
Outputs:
- query_grad: bfloat16 [12288, 2240], P(('tm', 'space'))
- key_grad: bfloat16 [12288, 2240], P(('tm', 'space'))
- value_grad: bfloat16 [12288, 2240], P(('tm', 'space'))
The draws below stay inside these ranges and needn't reach their ends.
All inputs are finite; a program needn't handle non-finite values.
Results may differ from the reference program's by a relative error of at most 0.003.
Values sent between devices are 32-bit elements; how exact they have to be, the bound alone decides.
No kernel may reach another device: no remote copies, remote signals or barrier semaphores. Data moves between devices by JAX's collectives and lax.ppermute only.
A program may use at most 64 MiB of HBM per device.

```python
import jax
import jax.numpy as jnp
from jax import lax

HEADS = 20
HEAD = 112
TOK_DEV = 384
WIDTH = 2240
TOKENS = 12288
N_TM = 2
N_SPACE = 16


def level_of(stream_key, dims, pieces, low, top_value):
    def one(position, shards_of):
        heights = jax.random.uniform(jax.random.fold_in(jax.random.fold_in(stream_key, 6), position), (shards_of,), jnp.float32, low / len(pieces), top_value / len(pieces))
        return jnp.repeat(jnp.exp(heights), dims[position] // shards_of).reshape((-1,) + (1,) * (len(dims) - position - 1))

    gain = one(*pieces[0])
    for cut in pieces[1:]:
        gain = gain * one(*cut)
    return gain


def bell_draw(rng, dims, scale, most, cuts=(), held_as=jnp.bfloat16):
    values = jax.random.normal(rng, dims, jnp.float32) * scale
    if len(cuts) > 0:
        values = level_of(rng, dims, cuts, -0.22, 0.18) * values
    return jnp.clip(values, min=-most, max=most).astype(held_as)


def setup_inputs(seed: int = 0) -> dict:
    seeds = jax.random.split(jax.random.key(seed), 5)
    return {
        "queries": bell_draw(seeds[0], (TOKENS, WIDTH), 1.0, 6.0, ((0, 32),)),
        "keys": bell_draw(seeds[1], (TOKENS, WIDTH), 1.0, 6.0, ((0, 32),)),
        "values": bell_draw(seeds[2], (TOKENS, WIDTH), 1.0, 6.0, ((0, 32),)),
        "out_grad": bell_draw(seeds[3], (TOKENS, WIDTH), ((HEAD * TOK_DEV * N_SPACE // 4) ** 0.5), 2560.0, ((0, 32),)),
    }


highest = lax.Precision.HIGHEST


def reference(queries, keys, values, out_grad):
    blocks = N_TM
    per_block = TOK_DEV * N_SPACE
    width = HEADS * HEAD

    def split(array):
        return array.reshape(blocks, per_block, HEADS, HEAD)

    query_blocks = split(queries)
    key_blocks = split(keys)
    value_blocks = split(values)
    grad_blocks = split(out_grad)

    def block_sums(items):
        key_block, value_block = items
        feat_key = jnp.maximum(key_block.astype(jnp.float32), 0.0)
        key_state = jnp.einsum("thi,thj->hij", feat_key, value_block.astype(jnp.float32), precision=highest)
        return key_state, jnp.sum(feat_key, axis=0)

    local_states, local_norms = lax.map(block_sums, (key_blocks, value_blocks))
    states = jnp.cumsum(local_states, axis=0)
    norms = jnp.cumsum(local_norms, axis=0)

    def query_side(items):
        query_block, grad_block, key_state, key_norm = items
        query_float = query_block.astype(jnp.float32)
        feat_query = jnp.maximum(query_float, 0.0)
        grad_heads = grad_block.astype(jnp.float32)
        numer = jnp.einsum("thi,hij->thj", feat_query, key_state, precision=highest)
        denom = jnp.einsum("thi,hi->th", feat_query, key_norm, precision=highest) + 1.0
        output = numer / denom[..., None]
        grad_numer = grad_heads / denom[..., None]
        grad_denom = -jnp.sum(grad_heads * output, axis=-1) / denom
        grad_feat = jnp.einsum("thj,hij->thi", grad_numer, key_state, precision=highest) + grad_denom[..., None] * key_norm[None]
        query_grad = jnp.where(query_float > 0, grad_feat, 0.0).astype(jnp.bfloat16)
        back_state = jnp.einsum("thi,thj->hij", feat_query, grad_numer, precision=highest)
        back_norm = jnp.sum(feat_query * grad_denom[..., None], axis=0)
        return query_grad, back_state, back_norm

    query_grads, back_states, back_norms = lax.map(query_side, (query_blocks, grad_blocks, states, norms))
    suffix_states = jnp.flip(jnp.cumsum(jnp.flip(back_states, 0), axis=0), 0)
    suffix_norms = jnp.flip(jnp.cumsum(jnp.flip(back_norms, 0), axis=0), 0)

    def key_side(items):
        key_block, value_block, grad_state, grad_norm = items
        key_float = key_block.astype(jnp.float32)
        feat_key = jnp.maximum(key_float, 0.0)
        value_float = value_block.astype(jnp.float32)
        value_grad = jnp.einsum("thi,hij->thj", feat_key, grad_state, precision=highest)
        key_feat = jnp.einsum("thj,hij->thi", value_float, grad_state, precision=highest) + grad_norm[None]
        key_grad = jnp.where(key_float > 0, key_feat, 0.0)
        return key_grad.astype(jnp.bfloat16), value_grad.astype(jnp.bfloat16)

    key_grads, value_grads = lax.map(key_side, (key_blocks, value_blocks, suffix_states, suffix_norms))
    total = blocks * per_block
    return (query_grads.reshape(total, width), key_grads.reshape(total, width), value_grads.reshape(total, width))
```

```python
import functools

import jax
import jax.numpy as jnp
from jax import lax
from jax.experimental import pallas as pl
from jax.experimental.pallas import tpu as pltpu
from jax.sharding import PartitionSpec as P

HEADS = 20
HEAD = 112
PIECES = 8

F32 = jnp.float32
BF16 = jnp.bfloat16


def runs_of(rows_piece):
    table = []
    for head in range(HEADS):
        row, end, runs = head * HEAD, (head + 1) * HEAD, []
        while row < end:
            piece = row // rows_piece
            stop = min(end, (piece + 1) * rows_piece)
            runs.append((piece, row - piece * rows_piece, row - head * HEAD, stop - row))
            row = stop
        table.append(runs)
    return table


def place_of(relative):
    return (relative & 1) * (PIECES // 2) + (relative >> 1)


def store_state(out_ref, head, state, mine):
    rows_piece = out_ref.shape[0] // PIECES
    for piece, offset, first, length in runs_of(rows_piece)[head]:
        start = pl.multiple_of(place_of(mine ^ piece) * rows_piece + offset, 8)
        out_ref[pl.ds(start, length), :] = state[first : first + length, :]


def split(x):
    high = x.astype(BF16)
    return high, (x - high.astype(F32)).astype(BF16)


def dot_nn(a, b):
    return lax.dot_general(a, b, (((1,), (0,)), ((), ())), preferred_element_type=F32)


def dot_nt(a, b):
    return lax.dot_general(a, b, (((1,), (1,)), ((), ())), preferred_element_type=F32)


def dot_tn(a, b):
    return lax.dot_general(a, b, (((0,), (0,)), ((), ())), preferred_element_type=F32)


def columns(head):
    return slice(head * HEAD, (head + 1) * HEAD)


def norm_kernel(k_ref, z_ref):
    feat = jnp.maximum(k_ref[...], 0)
    ones = jnp.ones((8, feat.shape[0]), BF16)
    z_ref[...] = dot_nn(ones, feat)[:1]


def state_kernel(mine_ref, k_ref, v_ref, s_ref):
    mine = mine_ref[0]
    for head in range(HEADS):
        feat = jnp.maximum(k_ref[:, columns(head)], 0)
        store_state(s_ref, head, dot_tn(feat, v_ref[:, columns(head)]), mine)


def denom_of(feat, z_row):
    high, low = split(jnp.broadcast_to(z_row, (HEAD, HEAD)))
    return dot_nt(feat, high) + dot_nt(feat, low) + 1.0


def back_kernel(mine_ref, q_ref, g_ref, z_ref, r_ref):
    mine = mine_ref[0]
    for head in range(HEADS):
        feat = jnp.maximum(q_ref[:, columns(head)], 0)
        denom = denom_of(feat, z_ref[:, columns(head)])
        high, low = split(g_ref[:, columns(head)].astype(F32) / denom)
        store_state(r_ref, head, dot_tn(feat, high) + dot_tn(feat, low), mine)


def unpack_state(mine, near_ref, far_ref, full_ref):
    rows_piece = full_ref.shape[0] // PIECES
    half = PIECES // 2
    for place in range(PIECES):
        ref, local = (near_ref, place) if place < half else (far_ref, place - half)
        relative = local * 2 + (place >= half)
        start = pl.multiple_of((mine ^ relative) * rows_piece, 8)
        full_ref[pl.ds(start, rows_piece), :] = ref[local * rows_piece : (local + 1) * rows_piece, :]


def query_kernel(mine_ref, q_ref, g_ref, z_ref, near_ref, far_ref, dq_ref, y_ref, full_ref):
    unpack_state(mine_ref[0], near_ref, far_ref, full_ref)
    ones = jnp.ones((HEAD, HEAD), BF16)
    for head in range(HEADS):
        query = q_ref[:, columns(head)]
        feat = jnp.maximum(query, 0)
        z_row = z_ref[:, columns(head)]
        inverse = 1.0 / denom_of(feat, z_row)
        s_high, s_low = split(full_ref[columns(head), :])
        grad = g_ref[:, columns(head)]
        pulled = dot_nt(grad, s_high) + dot_nt(grad, s_low)
        wide = feat.astype(F32)
        p_high, p_low = split(wide * pulled)
        inner = dot_nn(p_high, ones) + dot_nn(p_low, ones)
        grad_denom = -(inner * inverse) * inverse
        total = pulled * inverse + grad_denom * z_row
        dq_ref[:, columns(head)] = jnp.where(wide > 0, total, 0.0).astype(BF16)
        y_ref[:, columns(head)] = jnp.sum(wide * grad_denom, axis=0, keepdims=True)


def value_kernel(mine_ref, k_ref, near_ref, far_ref, dv_ref, full_ref):
    unpack_state(mine_ref[0], near_ref, far_ref, full_ref)
    for head in range(HEADS):
        feat = jnp.maximum(k_ref[:, columns(head)], 0)
        r_high, r_low = split(full_ref[columns(head), :])
        dv_ref[:, columns(head)] = (dot_nn(feat, r_high) + dot_nn(feat, r_low)).astype(BF16)


def key_kernel(mine_ref, k_ref, v_ref, y_ref, near_ref, far_ref, dk_ref, full_ref):
    unpack_state(mine_ref[0], near_ref, far_ref, full_ref)
    for head in range(HEADS):
        r_high, r_low = split(full_ref[columns(head), :])
        value = v_ref[:, columns(head)]
        pulled = dot_nt(value, r_high) + dot_nt(value, r_low) + y_ref[:, columns(head)]
        key = k_ref[:, columns(head)].astype(F32)
        dk_ref[:, columns(head)] = jnp.where(key > 0, pulled, 0.0).astype(BF16)


def call(kernel, name, outs, operands, scratch=(), flops=0):
    smem = pl.BlockSpec(memory_space=pltpu.SMEM)
    vmem = pl.BlockSpec(memory_space=pltpu.VMEM)
    moved = sum(o.size * o.dtype.itemsize for o in (*operands, *outs))
    return pl.pallas_call(
        kernel,
        name=name,
        out_shape=outs if len(outs) > 1 else outs[0],
        in_specs=[smem if o.dtype == jnp.int32 else vmem for o in operands],
        out_specs=[vmem] * len(outs) if len(outs) > 1 else vmem,
        scratch_shapes=list(scratch),
        cost_estimate=pl.CostEstimate(flops=flops, bytes_accessed=moved, transcendentals=0),
        compiler_params=pltpu.CompilerParams(vmem_limit_bytes=48 << 20),
    )(*operands)


def swap(x, size, distance):
    return lax.ppermute(x, "space", [(i, i ^ distance) for i in range(size)])


def across_blocks(x, blocks, reverse):
    position = lax.axis_index("tm")
    total = x
    for step in range(1, blocks):
        shift = -step if reverse else step
        other = lax.ppermute(x, "tm", [(i, (i + shift) % blocks) for i in range(blocks)])
        source = position - shift
        total = total + jnp.where((source >= 0) & (source < blocks), other, 0.0)
    return total


def sum_small(x, blocks, size, reverse):
    x = x + swap(x, size, 1)
    x = (x + swap(x, size, 2)) + (swap(x, size, 4) + swap(x, size, 6))
    total = x
    for far in range(1, size // PIECES):
        total = total + swap(x, size, far * PIECES)
    return across_blocks(total, blocks, reverse)


def sum_state(x, blocks, size, reverse):
    half = x.shape[0] // 2
    x = x[:half] + swap(x[half:], size, 1)
    rows = half // 4
    parts = [x[i * rows : (i + 1) * rows] for i in range(4)]
    x = (parts[0] + swap(parts[1], size, 2)) + (swap(parts[2], size, 4) + swap(parts[3], size, 6))
    total = x
    for far in range(1, size // PIECES):
        total = total + swap(x, size, far * PIECES)
    total = across_blocks(total, blocks, reverse)
    near = jnp.concatenate([total] + [swap(total, size, 2 * i) for i in range(1, 4)], axis=0)
    return near, swap(near, size, 1)


def on_device(blocks, size, queries, keys, values, out_grad):
    tokens, width = queries.shape
    mine = (lax.axis_index("space") % PIECES).astype(jnp.int32).reshape(1)
    row = jax.ShapeDtypeStruct((1, width), F32)
    state = jax.ShapeDtypeStruct((width, HEAD), F32)
    wide = jax.ShapeDtypeStruct((tokens, width), BF16)
    full = [pltpu.VMEM((width, HEAD), F32)]
    one = 2 * tokens * width * HEAD
    norm = call(norm_kernel, "norm", [row], (keys,), flops=one // 8)
    norm = sum_small(norm, blocks, size, False)
    local = call(state_kernel, "state", [state], (mine, keys, values), flops=one)
    near, far = sum_state(local, blocks, size, False)
    back = call(back_kernel, "back", [state], (mine, queries, out_grad, norm), flops=3 * one)
    back_near, back_far = sum_state(back, blocks, size, True)
    query_grad, bias = call(
        query_kernel, "query", [wide, row], (mine, queries, out_grad, norm, near, far), full, 6 * one
    )
    bias = sum_small(bias, blocks, size, True)
    value_grad = call(value_kernel, "value", [wide], (mine, keys, back_near, back_far), full, 2 * one)
    key_grad = call(
        key_kernel, "key", [wide], (mine, keys, values, bias, back_near, back_far), full, 2 * one
    )
    return query_grad, key_grad, value_grad


def solution(mesh):
    spec = P(("tm", "space"), None)
    return jax.shard_map(
        functools.partial(on_device, mesh.shape["tm"], mesh.shape["space"]),
        mesh=mesh,
        in_specs=(spec,) * 4,
        out_specs=(spec,) * 3,
        check_vma=False,
    )
```

```python
import functools

import jax
import jax.numpy as jnp
from jax import lax
from jax.experimental import pallas as pl
from jax.experimental.pallas import tpu as pltpu
from jax.sharding import PartitionSpec as P

HEADS = 20
HEAD = 112
PIECES = 8

F32 = jnp.float32
BF16 = jnp.bfloat16


LANES = 128
SUBLANES = 8


def relatives():
    return [place * 2 + core for core in (0, 1) for place in range(PIECES // 2)]


def send_pieces(mine, full_ref, piece_refs):
    rows = piece_refs[0].shape[0]
    for relative, ref in zip(relatives(), piece_refs):
        ref[...] = full_ref[pl.ds(pl.multiple_of((mine ^ relative) * rows, SUBLANES), rows), :]


def take_pieces(mine, piece_refs, full_ref):
    rows = piece_refs[0].shape[0]
    for relative, ref in zip(relatives(), piece_refs):
        full_ref[pl.ds(pl.multiple_of((mine ^ relative) * rows, SUBLANES), rows), :] = ref[...]


def split(x):
    high = x.astype(BF16)
    return high, (x - high.astype(F32)).astype(BF16)


def dot_nn(a, b):
    return lax.dot_general(a, b, (((1,), (0,)), ((), ())), preferred_element_type=F32)


def dot_nt(a, b):
    return lax.dot_general(a, b, (((1,), (1,)), ((), ())), preferred_element_type=F32)


def dot_tn(a, b):
    return lax.dot_general(a, b, (((0,), (0,)), ((), ())), preferred_element_type=F32)


def rows_of(head):
    return slice(head * HEAD, (head + 1) * HEAD)


def lane_pad(x):
    return jnp.concatenate([x, jnp.zeros((LANES - HEAD, x.shape[1]), x.dtype)], axis=0)


def norm_kernel(k_ref, z_ref):
    z_ref[...] = jnp.zeros_like(z_ref)
    ones = jnp.ones((SUBLANES, k_ref.shape[1]), BF16)
    for head in range(HEADS):
        feat = lane_pad(jnp.maximum(k_ref[rows_of(head), :], 0))
        z_ref[head : head + 1, :] = dot_nt(ones, feat)[:1]


def state_kernel(mine_ref, k_ref, v_ref, *refs):
    piece_refs, full_ref = refs[:-1], refs[-1]
    for head in range(HEADS):
        feat = jnp.maximum(k_ref[rows_of(head), :], 0)
        full_ref[rows_of(head), :] = dot_nt(feat, lane_pad(v_ref[rows_of(head), :]))
    send_pieces(mine_ref[0], full_ref, piece_refs)


def back_kernel(mine_ref, q_ref, g_ref, z_ref, inverse_ref, *refs):
    piece_refs, full_ref = refs[:-1], refs[-1]
    norms = z_ref[...].T
    inverse_ref[...] = jnp.zeros_like(inverse_ref)
    for head in range(HEADS):
        feat = jnp.maximum(q_ref[rows_of(head), :], 0)
        denom = jnp.sum(feat.astype(F32) * norms[:HEAD, head : head + 1], axis=0, keepdims=True) + 1.0
        inverse = 1.0 / denom
        inverse_ref[head : head + 1, :] = inverse
        high, low = split(g_ref[rows_of(head), :].astype(F32) * inverse)
        full_ref[rows_of(head), :] = dot_nt(feat, lane_pad(high)) + dot_nt(feat, lane_pad(low))
    send_pieces(mine_ref[0], full_ref, piece_refs)


def query_kernel(mine_ref, q_ref, g_ref, z_ref, inverse_ref, *refs):
    piece_refs, (dq_ref, y_ref, full_ref) = refs[:PIECES], refs[PIECES:]
    take_pieces(mine_ref[0], piece_refs, full_ref)
    norms = z_ref[...].T
    y_ref[...] = jnp.zeros_like(y_ref)
    for head in range(HEADS):
        query = q_ref[rows_of(head), :]
        feat = jnp.maximum(query, 0)
        wide = feat.astype(F32)
        inverse = inverse_ref[head : head + 1, :]
        high, low = split(full_ref[rows_of(head), :HEAD])
        grad = g_ref[rows_of(head), :]
        pulled = dot_nn(high, grad) + dot_nn(low, grad)
        inner = jnp.sum(wide * pulled, axis=0, keepdims=True)
        grad_denom = -(inner * inverse) * inverse
        total = pulled * inverse + grad_denom * norms[:HEAD, head : head + 1]
        dq_ref[rows_of(head), :] = jnp.where(wide > 0, total, 0.0).astype(BF16)
        high, low = split(jnp.broadcast_to(grad_denom, (SUBLANES, grad_denom.shape[1])))
        padded = lane_pad(feat)
        y_ref[head : head + 1, :] = (dot_nt(high, padded) + dot_nt(low, padded))[:1]


def value_kernel(mine_ref, k_ref, *refs):
    piece_refs, (dv_ref, full_ref) = refs[:PIECES], refs[PIECES:]
    take_pieces(mine_ref[0], piece_refs, full_ref)
    for head in range(HEADS):
        feat = jnp.maximum(k_ref[rows_of(head), :], 0)
        high, low = split(full_ref[rows_of(head), :HEAD])
        dv_ref[rows_of(head), :] = (dot_tn(high, feat) + dot_tn(low, feat)).astype(BF16)


def key_kernel(mine_ref, k_ref, v_ref, y_ref, *refs):
    piece_refs, (dk_ref, full_ref) = refs[:PIECES], refs[PIECES:]
    take_pieces(mine_ref[0], piece_refs, full_ref)
    bias = y_ref[...].T
    for head in range(HEADS):
        high, low = split(full_ref[rows_of(head), :HEAD])
        value = v_ref[rows_of(head), :]
        pulled = dot_nn(high, value) + dot_nn(low, value) + bias[:HEAD, head : head + 1]
        key = k_ref[rows_of(head), :].astype(F32)
        dk_ref[rows_of(head), :] = jnp.where(key > 0, pulled, 0.0).astype(BF16)


def call(kernel, name, outs, operands, scratch=(), flops=0):
    smem = pl.BlockSpec(memory_space=pltpu.SMEM)
    vmem = pl.BlockSpec(memory_space=pltpu.VMEM)
    moved = sum(o.size * o.dtype.itemsize for o in (*operands, *outs))
    return pl.pallas_call(
        kernel,
        name=name,
        out_shape=outs,
        in_specs=[smem if o.dtype == jnp.int32 else vmem for o in operands],
        out_specs=[vmem] * len(outs),
        scratch_shapes=list(scratch),
        cost_estimate=pl.CostEstimate(flops=flops, bytes_accessed=moved, transcendentals=0),
        compiler_params=pltpu.CompilerParams(vmem_limit_bytes=16 << 20),
    )(*operands)


def swap(x, size, distance):
    return lax.ppermute(x, "space", [(i, i ^ distance) for i in range(size)])


def across_blocks(x, blocks, reverse):
    position = lax.axis_index("tm")
    total = x
    for step in range(1, blocks):
        shift = -step if reverse else step
        other = lax.ppermute(x, "tm", [(i, (i + shift) % blocks) for i in range(blocks)])
        source = position - shift
        total = total + jnp.where((source >= 0) & (source < blocks), other, 0.0)
    return total


def across_space(parts, blocks, size, reverse):
    total = (parts[0] + swap(parts[1], size, 2)) + (swap(parts[2], size, 4) + swap(parts[3], size, 6))
    far = [swap(total, size, i * PIECES) for i in range(1, size // PIECES)]
    return across_blocks(sum(far, total), blocks, reverse)


def sum_small(x, blocks, size, reverse):
    return across_space([x + swap(x, size, 1)] * 4, blocks, size, reverse)


def sum_state(pieces, blocks, size, reverse):
    half = PIECES // 2
    parts = [near + swap(far, size, 1) for near, far in zip(pieces[:half], pieces[half:])]
    total = across_space(parts, blocks, size, reverse)
    near = [total] + [swap(total, size, 2 * i) for i in range(1, half)]
    return near + [swap(piece, size, 1) for piece in near]


def on_device(blocks, size, queries, keys, values, out_grad):
    queries, keys, values, out_grad = (x.T for x in (queries, keys, values, out_grad))
    width, tokens = queries.shape
    mine = (lax.axis_index("space") % PIECES).astype(jnp.int32).reshape(1)
    heads_up = -(-HEADS // SUBLANES) * SUBLANES
    row = jax.ShapeDtypeStruct((heads_up, LANES), F32)
    inverse = jax.ShapeDtypeStruct((heads_up, tokens), F32)
    pieces = [jax.ShapeDtypeStruct((width // PIECES, LANES), F32)] * PIECES
    wide = jax.ShapeDtypeStruct((width, tokens), BF16)
    full = [pltpu.VMEM((width, LANES), F32)]
    one = 2 * tokens * width * HEAD
    (norm,) = call(norm_kernel, "norm", [row], (keys,), flops=one // 8)
    norm = sum_small(norm, blocks, size, False)
    local = call(state_kernel, "state", pieces, (mine, keys, values), full, one)
    state = sum_state(local, blocks, size, False)
    inverse, *local = call(back_kernel, "back", [inverse, *pieces], (mine, queries, out_grad, norm), full, 2 * one)
    back = sum_state(local, blocks, size, True)
    query_grad, bias = call(
        query_kernel, "query", [wide, row], (mine, queries, out_grad, norm, inverse, *state), full, 3 * one
    )
    bias = sum_small(bias, blocks, size, True)
    (value_grad,) = call(value_kernel, "value", [wide], (mine, keys, *back), full, 2 * one)
    (key_grad,) = call(key_kernel, "key", [wide], (mine, keys, values, bias, *back), full, 2 * one)
    return query_grad.T, key_grad.T, value_grad.T


def solution(mesh):
    spec = P(("tm", "space"), None)
    return jax.shard_map(
        functools.partial(on_device, mesh.shape["tm"], mesh.shape["space"]),
        mesh=mesh,
        in_specs=(spec,) * 4,
        out_specs=(spec,) * 3,
        check_vma=False,
    )
```
